128 devices in a mesh: wide: 32 (over x, y, z_lo), narrow: 4 (over z_hi, core).
Axes of the slice: x: 4, y: 4, z: 4 (z_hi: 2, z_lo: 2; z = z_hi * 2 + z_lo), core: 2. Of those that a mesh axis runs over, the one named last changes fastest.
Arguments:
- mlp_input: bfloat16 [768, 5120], P('wide', 'narrow'), may hold values from -6 to 6
- grad_rows: bfloat16 [768, 5120], P('wide', 'narrow'), may hold values from -18 to 18
- enc_weight: bfloat16 [5120, 65536], P('narrow', 'wide'), may hold values from -0.078125 to 0.078125
- enc_bias: float32 [65536], P('wide'), may hold values from -3 to 3
- dec_weight: bfloat16 [65536, 5120], P('wide', 'narrow'), may hold values from -0.0234375 to 0.0234375
- dec_bias: float32 [5120], P('narrow'), may hold values from -3 to 3
Outputs:
- recon: bfloat16 [768, 5120], P('wide', 'narrow')
- attribution: bfloat16 [768, 65536], P(None, 'wide')
The draws below stay inside these ranges and needn't reach their ends.
All inputs are finite; a program needn't handle non-finite values.
Results may differ from the reference program's by a relative error of at most 0.023.
Values may be sent and summed in bfloat16 or wider, within the bound.
No kernel may reach another device: no remote copies, remote signals or barrier semaphores. Data moves between devices by JAX's collectives and lax.ppermute only.
A program may use at most 64 MiB of HBM per device.

```python
import jax
import jax.numpy as jnp
from jax import lax

D = 5120
LATENTS = 65536
TOKENS = 768
N_NARROW = 4


def block_levels(key, dims, cuts, least, high):
    factor_of = 1.0
    for axis_at, parts in cuts:
        steps = jax.random.uniform(jax.random.fold_in(jax.random.fold_in(key, 6), axis_at), (parts,), jnp.float32, least / len(cuts), high / len(cuts))
        factor_of = factor_of * jnp.repeat(jnp.exp(steps), dims[axis_at] // parts).reshape((-1,) + (1,) * (len(dims) - 1 - axis_at))
    return factor_of


def scatter_about(key, dims, scale, limit, shards=(), kind=jnp.bfloat16):
    gain = block_levels(key, dims, shards, -0.22, 0.18) if shards else 1.0
    drawn = jax.random.normal(key, dims, jnp.float32) * scale * gain
    return jnp.minimum(jnp.maximum(drawn, -limit), limit).astype(kind)


def setup_inputs(seed: int = 0) -> dict:
    keys = jax.random.split(jax.random.key(seed), 7)
    return {
        "mlp_input": scatter_about(keys[0], (TOKENS, D), 1.0, 6.0, ((0, 32), (1, 4))),
        "grad_rows": scatter_about(keys[1], (TOKENS, D), 3.0, 18.0, ((0, 32), (1, 4))),
        "enc_weight": scatter_about(keys[2], (D, LATENTS), D ** -0.5, 0.078125, ((0, 4), (1, 32))),
        "enc_bias": scatter_about(keys[3], (LATENTS,), 0.5, 3.0, ((0, 32),), jnp.float32),
        "dec_weight": scatter_about(keys[4], (LATENTS, D), LATENTS ** -0.5, 0.0234375, ((0, 32), (1, 4))),
        "dec_bias": scatter_about(keys[5], (D,), 0.5, 3.0, ((0, 4),), jnp.float32),
    }


def reference(mlp_input, grad_rows, enc_weight, enc_bias, dec_weight, dec_bias):
    block = D // N_NARROW
    rows = mlp_input.shape[0]
    pre = jnp.zeros((rows, LATENTS), jnp.float32)
    grad_proj = jnp.zeros((rows, LATENTS), jnp.float32)
    for index in range(N_NARROW):
        first = index * block
        enc_term = jnp.dot(mlp_input[:, first:first + block], enc_weight[first:first + block], preferred_element_type=jnp.float32)
        pre = pre + lax.optimization_barrier(enc_term.astype(jnp.bfloat16)).astype(jnp.float32)
        grad_term = jnp.dot(grad_rows[:, first:first + block], dec_weight[:, first:first + block].T, preferred_element_type=jnp.float32)
        grad_proj = grad_proj + lax.optimization_barrier(grad_term.astype(jnp.bfloat16)).astype(jnp.float32)
    latents = jnp.maximum(pre + enc_bias[None, :], 0.0).astype(jnp.bfloat16)
    attribution = (latents.astype(jnp.float32) * grad_proj).astype(jnp.bfloat16)
    recon = (jnp.dot(latents, dec_weight, preferred_element_type=jnp.float32) + dec_bias[None, :]).astype(jnp.bfloat16)
    return recon, attribution
```

```python
import jax
import jax.numpy as jnp
from jax import lax
from jax.sharding import Mesh
from jax.sharding import PartitionSpec as P


FLIP = [(0, 1), (1, 0)]
F32 = jnp.float32
BF16 = jnp.bfloat16


def shift(value, axis, by):
    return lax.ppermute(value, axis, [(i, (i + by) % 4) for i in range(4)])


def flip(value, axis):
    return lax.ppermute(value, axis, FLIP)


def dot(a, b):
    return jnp.dot(a, b, preferred_element_type=F32)


def dot_t(a, b):
    return lax.dot_general(a, b, (((1,), (1,)), ((), ())), preferred_element_type=F32)


def local(mlp_input, grad_rows, enc_weight, enc_bias, dec_weight, dec_bias):
    x, y, zl = lax.axis_index("x"), lax.axis_index("y"), lax.axis_index("zl")
    c = lax.axis_index("c")
    rows, width = mlp_input.shape
    latents = enc_weight.shape[1]
    half = latents // 2

    enc_own = lax.dynamic_slice(enc_weight, (0, c * half), (width, half))
    enc_oth = lax.dynamic_slice(enc_weight, (0, (1 - c) * half), (width, half))
    dec_own = lax.dynamic_slice(dec_weight, (c * half, 0), (half, width))
    dec_oth = lax.dynamic_slice(dec_weight, ((1 - c) * half, 0), (half, width))
    bias_own = lax.dynamic_slice(enc_bias, (c * half,), (half,))[None, :]
    enc_own, enc_oth, dec_own, dec_oth = lax.optimization_barrier((enc_own, enc_oth, dec_own, dec_oth))

    pair = jnp.stack([mlp_input, grad_rows])
    other = flip(pair, "zl")
    block = jnp.where(zl == 0, jnp.concatenate([pair, other], 1), jnp.concatenate([other, pair], 1))
    ring = [block] + [shift(block, "x", -k) for k in (1, 2, 3)]
    ring = jnp.stack(ring + ring[:3])
    gathered = lax.dynamic_slice(ring, ((4 - x) % 4, 0, 0, 0), (4, 2, 2 * rows, width))
    chunk_rows = 8 * rows
    feats = gathered[:, 0].reshape(chunk_rows, width)
    grads = gathered[:, 1].reshape(chunk_rows, width)

    def gather_y(v):
        return [v] + [shift(v, "y", k) for k in (1, 2, 3)]

    feat_chunks = gather_y(feats)
    grad_chunks = gather_y(grads)

    order = (0, 1, 3, 2)

    def pair_sum(v, own, oth, mul):
        sent = flip(mul(v, oth).astype(BF16), "c")
        return (mul(v, own) + sent.astype(F32)).astype(BF16)

    lat, rec = {}, {}
    for k in order:
        mine = pair_sum(feat_chunks[k], enc_own, enc_oth, dot)
        theirs = flip(mine, "zh")
        lat[k] = jnp.maximum(mine.astype(F32) + theirs.astype(F32) + bias_own, 0.0).astype(BF16)
        lat_oth = flip(lat[k], "c")
        rec[k] = (dot(lat[k], dec_own) + dot(lat_oth, dec_oth)).astype(BF16)

    summed = rec[0].astype(F32)
    for k in (1, 3, 2):
        summed = summed + shift(rec[k], "y", -k).astype(F32)
    pieces = summed.astype(BF16).reshape(4, 2 * rows, width)
    at = lambda j: lax.dynamic_index_in_dim(pieces, (x - j) % 4, 0, keepdims=False)
    summed = at(0).astype(F32)
    for j in (1, 3, 2):
        summed = summed + shift(at(j), "x", -j).astype(F32)
    summed = summed.astype(BF16)
    keep = lax.dynamic_slice(summed, (zl * rows, 0), (rows, width))
    send = lax.dynamic_slice(summed, ((1 - zl) * rows, 0), (rows, width))
    recon = (keep.astype(F32) + flip(send, "zl").astype(F32) + dec_bias[None, :]).astype(BF16)

    out = jnp.zeros((4, 4, 2 * rows, latents), BF16)
    for k in order:
        mine = pair_sum(grad_chunks[k], dec_own, dec_oth, dot_t)
        theirs = flip(mine, "zh")
        attr = (lat[k].astype(F32) * (mine.astype(F32) + theirs.astype(F32))).astype(BF16)
        attr_oth = flip(attr, "c")
        full = jnp.where(c == 0, jnp.concatenate([attr, attr_oth], 1), jnp.concatenate([attr_oth, attr], 1))
        out = lax.dynamic_update_slice(out, full.reshape(4, 1, 2 * rows, latents), (0, (y - k) % 4, 0, 0))
    return recon, out.reshape(32 * rows, latents)


def solution(mesh):
    fine = Mesh(mesh.devices.reshape(4, 4, 2, 2, 2), ("x", "y", "zl", "zh", "c"))
    wide, narrow = ("x", "y", "zl"), ("zh", "c")
    placed = (
        P(wide, narrow),
        P(wide, narrow),
        P(narrow, wide),
        P(wide),
        P(wide, narrow),
        P(narrow),
    )
    return jax.shard_map(
        local,
        mesh=fine,
        in_specs=placed,
        out_specs=(P(wide, narrow), P(None, wide)),
        check_vma=False,
    )
```
